32 devices in a mesh: groups: 2 (over y), seq: 8 (over z, x), width: 2 (over core).
Axes of the slice: x: 2, y: 2, z: 4, core: 2. Of those that a mesh axis runs over, the one named last changes fastest.
Arguments:
- span_tokens: bfloat16 [512, 16384], P(('groups', 'seq'), 'width'), parts along dimension 0, may hold values from -6 to 6
- kv_weight: bfloat16 [16384, 1024], P('seq', 'width'), may hold values from -0.046875 to 0.046875
- query_weight: bfloat16 [16384, 8192], P('seq', 'width'), may hold values from -0.046875 to 0.046875
- out_weight: bfloat16 [8192, 16384], P('width', 'seq'), may hold values from -6 to 6
- cache_keys: bfloat16 [16384, 4, 128], P(('groups', 'seq'), 'width'), parts along dimension 0, may hold values from -1000 to 1000
- cache_values: bfloat16 [16384, 4, 128], P(('groups', 'seq'), 'width'), parts along dimension 0, may hold values from -6 to 6
- hidden: bfloat16 [2, 64, 16384], P(None, 'groups', 'seq'), parts along dimension 1, may hold values from -6 to 6
- lengths: int32 [64], P('groups'), parts along dimension 0, may hold values from 1 to 8192
- offset: int32 [2], P('groups'), parts along dimension 0, may hold values from 4096 to 8192
Outputs:
- span_kv: bfloat16 [512, 1024], P(('groups', 'seq'), 'width'), parts along dimension 0
- attended: bfloat16 [2, 64, 16384], P(None, 'groups', ('seq', 'width')), parts along dimension 1
The draws below stay inside these ranges and needn't reach their ends.
There are 2 independent parts, one for each index of `groups`. The reference program is written for one: setup_inputs(seed, part) draws one part's arguments, and reference() takes and returns one part's arrays. A program takes and returns all parts, laid end to end along the dimension named above; an argument that names none is the same for every part. Nothing has to cross between parts.
All inputs are finite; a program needn't handle non-finite values.
Results may differ from the reference program's by a relative error of at most 0.014.
The reference program's roundings to bfloat16 on the way count: a program that leaves them out, or rounds other values in their place, can miss the bound.
Values may be sent and summed in bfloat16 or wider, within the bound.
A program may use at most 128 MiB of HBM per device.

```python
import math
import jax
import jax.numpy as jnp
from jax import lax

D = 16384
HD = 128
QH = 64
KVH = 4
STEPS = 2
BRANCHES = 32
TOK_DEV = 32
KEY_BLOCK = 256
SPAN = 256
CACHE = 8192


def draw_cache_keys(key, part):
    extent = (CACHE, KVH, HD)
    drawn = jax.random.normal(jax.random.fold_in(key, 11), extent, jnp.float32)
    return drawn.astype(jnp.bfloat16)


def plant(entries, rng, low, top_value):
    place = [jax.random.randint(jax.random.fold_in(rng, axis), (), 0, length) for axis, length in enumerate(entries.shape)]
    widest = entries.shape.index(max(entries.shape))
    beside = place[:widest] + [(place[widest] + 1) % entries.shape[widest]] + place[widest + 1:]
    return entries.at[tuple(place)].set(low).at[tuple(beside)].set(top_value)


def level_of(own_key, shape, shards, least, largest):
    level = 1.0
    for position, blocks in shards:
        heights = jax.random.uniform(jax.random.fold_in(jax.random.fold_in(own_key, 6), position), (blocks,), jnp.float32, least / len(shards), largest / len(shards))
        level = level * jnp.repeat(jnp.exp(heights), shape[position] // blocks).reshape((-1,) + (1,) * (len(shape) - 1 - position))
    return level


def normal_values(rng, shape, deviation, bound, cuts=(), held_as=jnp.bfloat16):
    factor_of = level_of(rng, shape, cuts, -0.22, 0.18) if cuts else 1.0
    values = jax.random.normal(rng, shape, jnp.float32) * deviation * factor_of
    return jnp.minimum(jnp.maximum(values, -bound), bound).astype(held_as)


def setup_inputs(seed: int = 0, part: int = 0) -> dict:
    seeds = jax.random.split(jax.random.key(seed), 10)
    part_splits = jax.random.split(jax.random.fold_in(seeds[9], part), 10)
    span_tokens = normal_values(part_splits[0], (SPAN, D), 1.0, 6.0, ((0, 8), (1, 2)))
    kv_weight = normal_values(seeds[1], (D, 2 * KVH * HD), D ** -0.5, 0.046875, ((0, 8), (1, 2)))
    query_weight = normal_values(seeds[2], (D, QH * HD), D ** -0.5, 0.046875, ((0, 8), (1, 2)))
    out_weight = normal_values(seeds[3], (QH * HD, D), 1.0, 6.0, ((0, 2), (1, 8)))
    cache_keys = draw_cache_keys(jax.random.fold_in(jax.random.fold_in(seeds[9], part), 71), part)
    cache_values = normal_values(part_splits[5], (CACHE, KVH, HD), 1.0, 6.0, ((0, 8), (1, 2)))
    hidden = normal_values(part_splits[6], (STEPS, BRANCHES, D), 1.0, 6.0, ((2, 8),))
    lengths = plant(jax.random.randint(part_splits[7], (BRANCHES,), 1, CACHE + 1), jax.random.fold_in(part_splits[7], 1), 1, CACHE).astype(jnp.int32)
    offset = jax.random.randint(part_splits[8], (1,), CACHE // 2, CACHE + 1).astype(jnp.int32)
    return {"span_tokens": span_tokens, "kv_weight": kv_weight, "query_weight": query_weight, "out_weight": out_weight, "cache_keys": cache_keys, "cache_values": cache_values, "hidden": hidden, "lengths": lengths, "offset": offset}


MASKED_SCORE = -1e+30

def combine(earlier, later):
    highest = jnp.maximum(earlier[0], later[0])
    keep_a = jnp.exp(earlier[0] - highest)
    keep_b = jnp.exp(later[0] - highest)
    return (highest, earlier[1] * keep_a + later[1] * keep_b, earlier[2] * keep_a[..., None] + later[2] * keep_b[..., None])

def weigh_block(scores, allowed):
    masked = jnp.where(allowed, scores, MASKED_SCORE)
    highest = lax.optimization_barrier(jnp.max(masked, axis=-1))
    weights = jnp.where(allowed, jnp.exp(masked - highest[..., None]), 0.0)
    return (highest, lax.optimization_barrier(jnp.sum(weights, axis=-1)), weights.astype(jnp.bfloat16))

def shared_block(queries, key_block, value_block, allowed, factor):
    scores = jnp.einsum('hqd,khd->hqk', queries, key_block.astype(jnp.float32)) * factor
    highest, weight_sum, weights = weigh_block(scores, allowed)
    summed = jnp.einsum('hqk,khd->hqd', weights.astype(jnp.float32), value_block.astype(jnp.float32))
    return (highest, weight_sum, summed)

def reference(span_tokens, kv_weight, query_weight, out_weight, cache_keys, cache_values, hidden, lengths, offset):
    factor = 1.0 / math.sqrt(HD)
    grouped = QH // KVH
    row_count = STEPS * BRANCHES
    flat_rows = row_count * grouped
    span_kv = jnp.dot(span_tokens, kv_weight, preferred_element_type=jnp.float32).astype(jnp.bfloat16)
    states = hidden.reshape(row_count, D)
    query_rows = jnp.dot(states, query_weight, preferred_element_type=jnp.float32).astype(jnp.bfloat16)
    fresh_rows = jnp.dot(states, kv_weight, preferred_element_type=jnp.float32).astype(jnp.bfloat16)
    queries = query_rows.reshape(row_count, KVH, grouped, HD).transpose(1, 0, 2, 3).reshape(KVH, flat_rows, HD)
    queries = queries.astype(jnp.float32)
    visible = jnp.minimum(lengths, offset[0])
    visible_flat = jnp.repeat(jnp.tile(visible, STEPS), grouped)
    start_state = (jnp.full((KVH, flat_rows), MASKED_SCORE, jnp.float32), jnp.zeros((KVH, flat_rows), jnp.float32), jnp.zeros((KVH, flat_rows, HD), jnp.float32))

    def cache_step(running, block_id):
        leading = block_id * KEY_BLOCK
        key_block = lax.dynamic_slice_in_dim(cache_keys, leading, KEY_BLOCK, 0)
        value_block = lax.dynamic_slice_in_dim(cache_values, leading, KEY_BLOCK, 0)
        places = leading + jnp.arange(KEY_BLOCK, dtype=jnp.int32)
        allowed = (places[None, :] < visible_flat[:, None])[None]
        return (combine(running, shared_block(queries, key_block, value_block, allowed, factor)), None)
    running, unused = lax.scan(cache_step, start_state, jnp.arange(CACHE // KEY_BLOCK, dtype=jnp.int32))
    span_pairs = span_kv.reshape(SPAN, KVH, 2, HD)
    everywhere = jnp.ones((1, 1, 1), jnp.bool_)

    def span_step(running, block_id):
        leading = block_id * TOK_DEV
        pairs = lax.dynamic_slice_in_dim(span_pairs, leading, TOK_DEV, 0)
        return (combine(running, shared_block(queries, pairs[:, :, 0], pairs[:, :, 1], everywhere, factor)), None)
    running, unused = lax.scan(span_step, running, jnp.arange(SPAN // TOK_DEV, dtype=jnp.int32))
    grid = query_rows.reshape(STEPS, BRANCHES, KVH, grouped, HD).astype(jnp.float32)
    fresh_pairs = fresh_rows.reshape(STEPS, BRANCHES, KVH, 2, HD).astype(jnp.float32)
    self_scores = jnp.einsum('tbhgd,ubhd->htbgu', grid, fresh_pairs[:, :, :, 0]) * factor
    self_scores = self_scores.reshape(KVH, flat_rows, STEPS)
    causal = jnp.arange(STEPS)[None, :] <= jnp.arange(STEPS)[:, None]
    allowed = jnp.broadcast_to(causal[:, None, None, :], (STEPS, BRANCHES, grouped, STEPS)).reshape(flat_rows, STEPS)[None]
    highest, weight_sum, weights = weigh_block(self_scores, allowed)
    weights = weights.reshape(KVH, STEPS, BRANCHES, grouped, STEPS).astype(jnp.float32)
    summed = jnp.einsum('htbgu,ubhd->htbgd', weights, fresh_pairs[:, :, :, 1]).reshape(KVH, flat_rows, HD)
    finished = combine(running, (highest, weight_sum, summed))
    attention = (finished[2] / finished[1][..., None]).astype(jnp.bfloat16)
    attention = attention.reshape(KVH, row_count, grouped, HD).transpose(1, 0, 2, 3).reshape(row_count, QH * HD)
    attended = jnp.dot(attention, out_weight, preferred_element_type=jnp.float32).astype(jnp.bfloat16)
    return (span_kv, attended.reshape(STEPS, BRANCHES, D))
```

```python
import functools
import math

import jax
import jax.numpy as jnp
from jax import lax
from jax.experimental import pallas as pl
from jax.experimental.pallas import tpu as pltpu
from jax.sharding import PartitionSpec as P

HD = 128
QH = 64
KVH = 4
MASKED = -1e30
MESH = pl.DeviceIdType.MESH
NT = (((1,), (1,)), ((), ()))


def remote(src, dst, send, recv, device):
    return pltpu.make_async_remote_copy(
        src_ref=src, dst_ref=dst, send_sem=send, recv_sem=recv, device_id=device, device_id_type=MESH
    )


def layer(
    n, steps, tile,
    tok_ref, hid_ref, vis_ref, kvw_ref, qw_ref, ow_ref, ck_ref, cv_ref,
    span_ref, out_ref,
    qw_v, kvw_v, ow_v, ck_v, cv_v, vt_v, vts_v,
    part, qrecv, tokg, spart, srecv, gath, obuf, orecv, mlbuf, mlrecv, att, xbuf, xrecv,
    qw_sem, kvw_sem, ow_sem, c_sem, own_sem,
    tok_s, tok_r, fwd_s, q_s, q_r, sp_s, sp_r, g_s, g_r, o_s, o_r, ml_s, ml_r, a_s, a_r, x_s, x_r,
):
    f32, bf16 = jnp.float32, jnp.bfloat16
    me = lax.axis_index("seq")
    w = lax.axis_index("width")
    other = 1 - w
    r = part.shape[1]
    heads = kvw_v.shape[1] // (2 * HD)
    grouped = QH // KVH
    qcols = qw_ref.shape[1]
    ccols = part.shape[2]
    tiles = qcols // tile
    feats = hid_ref.shape[1]
    lanes = grouped * r
    factor = 1.0 / math.sqrt(HD)
    per_half = tok_ref.shape[1] // feats
    toks = tok_ref.shape[0]

    def peers(body):
        def step(d, carry):
            body(lax.rem(me + d, n))
            return carry

        lax.fori_loop(1, n, step, 0)

    def qw_copy(t):
        cols = pl.ds(pl.multiple_of(t * tile, tile), tile)
        return pltpu.make_async_copy(qw_ref.at[:, cols], qw_v.at[t], qw_sem.at[t])

    for t in range(tiles):
        qw_copy(t).start()
    kvw_copy = pltpu.make_async_copy(kvw_ref, kvw_v, kvw_sem)
    kvw_copy.start()
    ck_copy = pltpu.make_async_copy(ck_ref, ck_v, c_sem.at[0])
    cv_copy = pltpu.make_async_copy(cv_ref, cv_v, c_sem.at[1])
    ck_copy.start()
    cv_copy.start()
    ow_parts = ow_sem.shape[0]
    ow_rows = ow_ref.shape[0] // ow_parts
    ow_copies = [
        pltpu.make_async_copy(
            ow_ref.at[pl.ds(k * ow_rows, ow_rows)], ow_v.at[pl.ds(k * ow_rows, ow_rows)], ow_sem.at[k]
        )
        for k in range(ow_parts)
    ]
    for copy in ow_copies:
        copy.start()

    barrier = pltpu.get_barrier_semaphore()
    peers(
        lambda j: pl.semaphore_signal(barrier, inc=1, device_id={"seq": j}, device_id_type=MESH)
    )
    pl.semaphore_signal(barrier, inc=1, device_id={"width": other}, device_id_type=MESH)
    pl.semaphore_wait(barrier, n)

    def tok_copy(k):
        dest = w * per_half + k
        cols = pl.ds(pl.multiple_of(k * feats, 128), feats)
        return dest, cols

    def tok_send(k, carry):
        dest, cols = tok_copy(k)

        @pl.when(dest != me)
        def _():
            remote(
                tok_ref.at[:, cols], tokg.at[me], tok_s.at[k], tok_r.at[me], {"seq": dest}
            ).start()

        @pl.when(dest == me)
        def _():
            pltpu.make_async_copy(tok_ref.at[:, cols], tokg.at[me], own_sem).start()

        return carry

    lax.fori_loop(0, per_half, tok_send, 0)

    def q_send(value, cols):
        for j in range(n):
            part[j, :, cols] = value[j * r : (j + 1) * r]
        peers(
            lambda j: remote(
                part.at[j, :, cols], qrecv.at[me, :, cols], q_s.at[j], q_r.at[me], {"seq": j}
            ).start()
        )

    def q_tile(t, carry):
        qw_copy(t).wait()
        value = jnp.dot(hid_ref[...], qw_v[t], preferred_element_type=f32)
        q_send(value, pl.ds(pl.multiple_of(t * tile, tile), tile))
        return carry

    lax.fori_loop(0, tiles, q_tile, 0)
    kvw_copy.wait()
    q_send(
        jnp.dot(hid_ref[...], kvw_v[...], preferred_element_type=f32), pl.ds(qcols, ccols - qcols)
    )

    holder = w == me // per_half

    def tok_recv(i, device):
        return remote(tokg.at[i], tokg.at[i], fwd_s.at[i], tok_r.at[i], device)

    @pl.when(holder)
    def _():
        pltpu.make_async_copy(tokg.at[me], tokg.at[me], own_sem).wait()

        def pass_on(d, carry):
            i = lax.rem(me + d, n)

            @pl.when(i != me)
            def _():
                tok_recv(i, {"seq": i}).wait_recv()

            tok_recv(i, {"width": other}).start()
            return carry

        lax.fori_loop(0, n, pass_on, 0)

    @pl.when(jnp.logical_not(holder))
    def _():
        def take(i, carry):
            tok_recv(i, {"width": other}).wait_recv()
            return carry

        lax.fori_loop(0, n, take, 0)

    group = min(n, 8)

    def span_chunk(c, carry):
        rows = tokg[pl.ds(c * group, group)].reshape(group * toks, feats)
        value = jnp.dot(rows, kvw_v[...], preferred_element_type=f32)
        spart[pl.ds(c * group, group)] = value.reshape(group, toks, value.shape[1])
        return carry

    lax.fori_loop(0, n // group, span_chunk, 0)
    peers(
        lambda j: remote(spart.at[j], srecv.at[me], sp_s.at[j], sp_r.at[me], {"seq": j}).start()
    )

    qrecv[me] = part[me]
    peers(lambda j: remote(part.at[j], qrecv.at[j], q_s.at[j], q_r.at[j], {"seq": j}).wait_recv())
    total = lax.fori_loop(1, n, lambda i, acc: acc + qrecv[i], qrecv[0])
    gath[me] = jnp.concatenate(
        [total[:, c * HD : (c + 1) * HD] for c in range(ccols // HD)], axis=0
    ).astype(bf16)
    peers(lambda j: remote(gath.at[me], gath.at[me], g_s.at[j], g_r.at[me], {"seq": j}).start())

    ck_copy.wait()
    cv_copy.wait()
    for h in range(heads):
        vt_v[h] = cv_v[:, h * HD : (h + 1) * HD].astype(f32).T.astype(bf16)

    srecv[me] = spart[me]
    peers(lambda j: remote(spart.at[j], srecv.at[j], sp_s.at[j], sp_r.at[j], {"seq": j}).wait_recv())
    span = lax.fori_loop(1, n, lambda i, acc: acc + srecv[i], srecv[0]).astype(bf16)
    span_ref[...] = span
    for h in range(heads):
        vts_v[h] = span[:, (2 * h + 1) * HD : (2 * h + 2) * HD].astype(f32).T.astype(bf16)

    peers(lambda j: remote(gath.at[j], gath.at[j], g_s.at[j], g_r.at[j], {"seq": j}).wait_recv())

    slots = ck_v.shape[0]
    anchor = me * slots
    jc = max(1, min(n, 256 // lanes))
    width = jc * lanes

    def attend(c, carry):
        visible = vis_ref[pl.ds(c, 1)] - anchor
        for h in range(heads):
            q = gath[pl.ds(c * jc, jc), h * lanes : (h + 1) * lanes, :].reshape(width, HD)
            s1 = lax.dot_general(
                ck_v[:, h * HD : (h + 1) * HD], q, NT, preferred_element_type=f32
            ) * factor
            s2 = lax.dot_general(
                span_ref[:, 2 * h * HD : (2 * h + 1) * HD], q, NT, preferred_element_type=f32
            ) * factor
            place = lax.broadcasted_iota(jnp.int32, s1.shape, 0)
            s1 = jnp.where(place < visible, s1, MASKED)
            m = jnp.maximum(
                jnp.max(s1, axis=0, keepdims=True), jnp.max(s2, axis=0, keepdims=True)
            )
            w1 = jnp.exp(s1 - m)
            w2 = jnp.exp(s2 - m)
            l = jnp.sum(w1, axis=0, keepdims=True) + jnp.sum(w2, axis=0, keepdims=True)
            o = jnp.dot(vt_v[h], w1.astype(bf16), preferred_element_type=f32)
            o = (o + jnp.dot(vts_v[h], w2.astype(bf16), preferred_element_type=f32)).astype(bf16)
            for k in range(jc):
                cut = slice(k * lanes, (k + 1) * lanes)
                obuf[c * jc + k, h] = o[:, cut]
                mlbuf[c * jc + k, h : h + 1] = m[:, cut]
                mlbuf[c * jc + k, heads + h : heads + h + 1] = l[:, cut]
        for k in range(jc):
            j = c * jc + k

            @pl.when(j != me)
            def _():
                remote(mlbuf.at[j], mlrecv.at[me], ml_s.at[j], ml_r.at[me], {"seq": j}).start()
                remote(obuf.at[j], orecv.at[me], o_s.at[j], o_r.at[me], {"seq": j}).start()

        return carry

    lax.fori_loop(0, n // jc, attend, 0)

    per_step = n // steps
    step = me // per_step
    fresh = []
    for h in range(heads):
        q = gath[me, h * lanes : (h + 1) * lanes, :]
        base = (heads * grouped + 2 * h) * r
        pairs = [
            gath[u * per_step + lax.rem(me, per_step)].astype(f32) for u in range(steps)
        ]
        keys = jnp.concatenate([p[base : base + r] for p in pairs], axis=0)
        values = jnp.concatenate([p[base + r : base + 2 * r] for p in pairs], axis=0)
        s = lax.dot_general(keys.astype(bf16), q, NT, preferred_element_type=f32) * factor
        row = lax.broadcasted_iota(jnp.int32, s.shape, 0)
        lane = lax.broadcasted_iota(jnp.int32, s.shape, 1)
        allowed = jnp.logical_and(lax.rem(row, r) == lax.rem(lane, r), row // r <= step)
        s = jnp.where(allowed, s, MASKED)
        m = jnp.max(s, axis=0, keepdims=True)
        e = jnp.where(allowed, jnp.exp(s - m), 0.0)
        l = jnp.sum(e, axis=0, keepdims=True)
        o = jnp.dot(values.T.astype(bf16), e.astype(bf16), preferred_element_type=f32)
        fresh.append((m, l, o))

    orecv[me] = obuf[me]
    mlrecv[me] = mlbuf[me]

    def o_wait(j):
        remote(mlbuf.at[j], mlrecv.at[j], ml_s.at[j], ml_r.at[j], {"seq": j}).wait_recv()
        remote(obuf.at[j], orecv.at[j], o_s.at[j], o_r.at[j], {"seq": j}).wait_recv()

    peers(o_wait)
    pieces = []
    for h in range(heads):
        m0, l0, o0 = fresh[h]
        top = lax.fori_loop(0, n, lambda i, a: jnp.maximum(a, mlrecv[i, h : h + 1]), m0)
        keep = jnp.exp(m0 - top)

        def fold(i, acc):
            k = jnp.exp(mlrecv[i, h : h + 1] - top)
            return acc[0] + mlrecv[i, heads + h : heads + h + 1] * k, acc[1] + orecv[i, h].astype(f32) * k

        l, o = lax.fori_loop(0, n, fold, (l0 * keep, o0 * keep))
        ready = (o / l).T
        pieces += [ready[g * r : (g + 1) * r] for g in range(grouped)]
    att[me] = jnp.concatenate(pieces, axis=1).astype(bf16)
    peers(lambda j: remote(att.at[me], att.at[me], a_s.at[j], a_r.at[me], {"seq": j}).start())
    for copy in ow_copies:
        copy.wait()
    peers(lambda j: remote(att.at[j], att.at[j], a_s.at[j], a_r.at[j], {"seq": j}).wait_recv())
    rows = jnp.concatenate([att[j].astype(f32) for j in range(n)], axis=0).astype(bf16)
    own = out_ref.shape[1]
    cut = min(own, 256)

    def out_tile(side, c):
        cols = pl.ds(pl.multiple_of(side * own + c * cut, 128), cut)
        return jnp.dot(rows, ow_v[:, cols], preferred_element_type=f32)

    for c in range(own // cut):
        xbuf[:, c * cut : (c + 1) * cut] = out_tile(other, c).astype(bf16)
    swap = remote(xbuf, xrecv, x_s, x_r, {"width": other})
    swap.start()
    kept = [out_tile(w, c) for c in range(own // cut)]
    swap.wait_recv()
    for c in range(own // cut):
        there = slice(c * cut, (c + 1) * cut)
        out_ref[:, there] = (kept[c] + xrecv[:, there].astype(f32)).astype(bf16)

    def tok_sent(k, carry):
        dest, cols = tok_copy(k)

        @pl.when(dest != me)
        def _():
            remote(
                tok_ref.at[:, cols], tokg.at[me], tok_s.at[k], tok_r.at[me], {"seq": dest}
            ).wait_send()

        return carry

    lax.fori_loop(0, per_half, tok_sent, 0)

    @pl.when(holder)
    def _():
        def passed(i, carry):
            tok_recv(i, {"width": other}).wait_send()
            return carry

        lax.fori_loop(0, n, passed, 0)

    def sent(j):
        at = {"seq": j}
        remote(part.at[j], qrecv.at[me], q_s.at[j], q_r.at[me], at).wait_send()
        remote(spart.at[j], srecv.at[me], sp_s.at[j], sp_r.at[me], at).wait_send()
        remote(gath.at[me], gath.at[me], g_s.at[j], g_r.at[me], at).wait_send()
        remote(mlbuf.at[j], mlrecv.at[me], ml_s.at[j], ml_r.at[me], at).wait_send()
        remote(obuf.at[j], orecv.at[me], o_s.at[j], o_r.at[me], at).wait_send()
        remote(att.at[me], att.at[me], a_s.at[j], a_r.at[me], at).wait_send()

    peers(sent)
    swap.wait_send()


def local(
    mesh,
    span_tokens, kv_weight, query_weight, out_weight, cache_keys, cache_values, hidden, lengths, offset,
):
    n = mesh.shape["seq"]
    steps, branches, feats = hidden.shape
    rows = steps * branches
    r = rows // n
    grouped = QH // KVH
    lanes = grouped * r
    toks = span_tokens.shape[0]
    kvc = kv_weight.shape[1]
    heads = kvc // (2 * HD)
    qcols = query_weight.shape[1]
    ccols = qcols + kvc
    tile = min(qcols, 512)
    slots = cache_keys.shape[0]
    own = out_weight.shape[1] // mesh.shape["width"]
    f32, bf16 = jnp.float32, jnp.bfloat16

    jc = max(1, min(n, 256 // lanes))
    visible = jnp.tile(jnp.minimum(lengths, offset[0]), steps).reshape(n, 1, r)
    visible = jnp.broadcast_to(visible, (n, grouped, r)).reshape(n // jc, jc * lanes)

    vm = pl.BlockSpec(memory_space=pltpu.VMEM)
    hbm = pl.BlockSpec(memory_space=pl.ANY)
    dma = pltpu.SemaphoreType.DMA
    ow_parts = 8
    span_kv, out = pl.pallas_call(
        functools.partial(layer, n, steps, tile),
        out_shape=(
            jax.ShapeDtypeStruct((toks, kvc), bf16),
            jax.ShapeDtypeStruct((rows, own), bf16),
        ),
        in_specs=[vm, vm, vm, hbm, hbm, hbm, hbm, hbm],
        out_specs=(vm, vm),
        scratch_shapes=[
            pltpu.VMEM((qcols // tile, feats, tile), bf16),
            pltpu.VMEM((feats, kvc), bf16),
            pltpu.VMEM(out_weight.shape, bf16),
            pltpu.VMEM((slots, heads * HD), bf16),
            pltpu.VMEM((slots, heads * HD), bf16),
            pltpu.VMEM((heads, HD, slots), bf16),
            pltpu.VMEM((heads, HD, toks), bf16),
            pltpu.VMEM((n, r, ccols), f32),
            pltpu.VMEM((n, r, ccols), f32),
            pltpu.VMEM((n, toks, feats), bf16),
            pltpu.VMEM((n, toks, kvc), f32),
            pltpu.VMEM((n, toks, kvc), f32),
            pltpu.VMEM((n, ccols // HD * r, HD), bf16),
            pltpu.VMEM((n, heads, HD, lanes), bf16),
            pltpu.VMEM((n, heads, HD, lanes), bf16),
            pltpu.VMEM((n, 2 * heads, lanes), f32),
            pltpu.VMEM((n, 2 * heads, lanes), f32),
            pltpu.VMEM((n, r, qcols), bf16),
            pltpu.VMEM((rows, own), bf16),
            pltpu.VMEM((rows, own), bf16),
            dma((qcols // tile,)), dma, dma((ow_parts,)), dma((2,)), dma,
            dma((n,)), dma((n,)), dma((n,)), dma((n,)), dma((n,)), dma((n,)), dma((n,)),
            dma((n,)), dma((n,)), dma((n,)), dma((n,)), dma((n,)), dma((n,)), dma((n,)), dma((n,)),
            dma, dma,
        ],
        compiler_params=pltpu.CompilerParams(
            collective_id=0, has_side_effects=True, vmem_limit_bytes=62 * 1024 * 1024
        ),
    )(
        span_tokens,
        hidden.reshape(rows, feats),
        visible,
        kv_weight,
        query_weight,
        out_weight,
        cache_keys.reshape(slots, heads * HD),
        cache_values.reshape(slots, heads * HD),
    )
    return span_kv, out.reshape(steps, branches, own)


def solution(mesh):
    return jax.shard_map(
        functools.partial(local, mesh),
        mesh=mesh,
        in_specs=(
            P(("groups", "seq"), "width"),
            P("seq", "width"),
            P("seq", "width"),
            P("width", "seq"),
            P(("groups", "seq"), "width", None),
            P(("groups", "seq"), "width", None),
            P(None, "groups", "seq"),
            P("groups"),
            P("groups"),
        ),
        out_specs=(P(("groups", "seq"), "width"), P(None, "groups", ("seq", "width"))),
        check_vma=False,
    )
```

```python
import functools
import math

import jax
import jax.numpy as jnp
from jax import lax
from jax.experimental import pallas as pl
from jax.experimental.pallas import tpu as pltpu
from jax.sharding import PartitionSpec as P

HD = 128
QH = 64
KVH = 4
MASKED = -1e30
MESH = pl.DeviceIdType.MESH
NT = (((1,), (1,)), ((), ()))


def remote(src, dst, send, recv, device):
    return pltpu.make_async_remote_copy(
        src_ref=src, dst_ref=dst, send_sem=send, recv_sem=recv, device_id=device, device_id_type=MESH
    )


def layer(
    n, steps, tile,
    tok_ref, hid_ref, vis_ref, kvw_ref, qw_ref, ow_ref, ck_ref, cv_ref,
    span_ref, out_ref,
    qw_v, kvw_v, ow_v, ck_v, cv_v, vt_v, vts_v,
    part, qpair, qrecv, tokg, spart, spair, srecv, gath, oacc, mlacc,
    obuf, orecv, mlbuf, mlrecv, att, xbuf, xrecv,
    qw_sem, kvw_sem, ow_sem, c_sem, own_sem,
    tok_s, tok_r, fwd_s, qp_s, qp_r, q_s, q_r, spp_s, spp_r, sp_s, sp_r,
    g_s, g_r, gp_s, o_s, o_r, ml_s, ml_r, a_s, a_r, ap_s, x_s, x_r,
):
    f32, bf16 = jnp.float32, jnp.bfloat16
    me = lax.axis_index("seq")
    w = lax.axis_index("width")
    other = 1 - w
    parity, col, half = lax.rem(me, 2), me // 2, n // 2
    pair = me + 1 - 2 * parity
    r = part.shape[2]
    heads = kvw_v.shape[1] // (2 * HD)
    grouped = QH // KVH
    qcols = qw_ref.shape[1]
    ccols = part.shape[3]
    tiles = qcols // tile
    feats = hid_ref.shape[1]
    lanes = grouped * r
    factor = 1.0 / math.sqrt(HD)
    per_half = tok_ref.shape[1] // feats
    toks = tok_ref.shape[0]

    def peers(body):
        def step(d, carry):
            body(lax.rem(me + d, n))
            return carry

        lax.fori_loop(1, n, step, 0)

    def mates(body):
        def step(d, carry):
            k = lax.rem(col + d, half)
            body(k, 2 * k + parity)
            return carry

        lax.fori_loop(1, half, step, 0)

    def spread(buf, send, pass_on, recv):
        at_pair = {"seq": pair}
        mates(lambda k, j: remote(buf.at[me], buf.at[me], send.at[k], recv.at[me], {"seq": j}).start())
        remote(buf.at[me], buf.at[me], pass_on.at[col], recv.at[me], at_pair).start()

    def relay(buf, send, pass_on, recv):
        def one(k, j):
            remote(buf.at[j], buf.at[j], send.at[k], recv.at[j], {"seq": j}).wait_recv()
            remote(buf.at[j], buf.at[j], pass_on.at[k], recv.at[j], {"seq": pair}).start()

        mates(one)

    def collect(buf, pass_on, recv):
        def one(k, carry):
            j = 2 * k + 1 - parity
            remote(buf.at[j], buf.at[j], pass_on.at[k], recv.at[j], {"seq": pair}).wait_recv()
            return carry

        lax.fori_loop(0, half, one, 0)

    def spread_sent(buf, send, pass_on, recv):
        mates(
            lambda k, j: remote(buf.at[me], buf.at[me], send.at[k], recv.at[me], {"seq": j}).wait_send()
        )

        def one(k, carry):
            j = 2 * k + parity
            remote(buf.at[j], buf.at[j], pass_on.at[k], recv.at[j], {"seq": pair}).wait_send()
            return carry

        lax.fori_loop(0, half, one, 0)

    def qw_copy(t):
        cols = pl.ds(pl.multiple_of(t * tile, tile), tile)
        return pltpu.make_async_copy(qw_ref.at[:, cols], qw_v.at[t], qw_sem.at[t])

    for t in range(tiles):
        qw_copy(t).start()
    kvw_copy = pltpu.make_async_copy(kvw_ref, kvw_v, kvw_sem)
    kvw_copy.start()
    ck_copy = pltpu.make_async_copy(ck_ref, ck_v, c_sem.at[0])
    cv_copy = pltpu.make_async_copy(cv_ref, cv_v, c_sem.at[1])
    ck_copy.start()
    cv_copy.start()
    ow_parts = ow_sem.shape[0]
    ow_rows = ow_ref.shape[0] // ow_parts
    ow_copies = [
        pltpu.make_async_copy(
            ow_ref.at[pl.ds(k * ow_rows, ow_rows)], ow_v.at[pl.ds(k * ow_rows, ow_rows)], ow_sem.at[k]
        )
        for k in range(ow_parts)
    ]
    for copy in ow_copies:
        copy.start()

    barrier = pltpu.get_barrier_semaphore()
    peers(
        lambda j: pl.semaphore_signal(barrier, inc=1, device_id={"seq": j}, device_id_type=MESH)
    )
    pl.semaphore_signal(barrier, inc=1, device_id={"width": other}, device_id_type=MESH)
    pl.semaphore_wait(barrier, n)

    def tok_copy(k):
        dest = w * per_half + k
        cols = pl.ds(pl.multiple_of(k * feats, 128), feats)
        return dest, cols

    def tok_send(k, carry):
        dest, cols = tok_copy(k)

        @pl.when(dest != me)
        def _():
            remote(
                tok_ref.at[:, cols], tokg.at[parity, col], tok_s.at[k], tok_r.at[me], {"seq": dest}
            ).start()

        @pl.when(dest == me)
        def _():
            pltpu.make_async_copy(tok_ref.at[:, cols], tokg.at[parity, col], own_sem).start()

        return carry

    lax.fori_loop(0, per_half, tok_send, 0)

    def span_cols(t):
        return pl.ds(pl.multiple_of(t * tile, tile), tile)

    def pair_copy(t):
        cols = span_cols(t)
        return remote(
            part.at[1 - parity, :, :, cols], qpair.at[:, :, cols], qp_s.at[t], qp_r.at[t], {"seq": pair}
        )

    def q_send(value, t):
        cols = span_cols(t)
        for j in range(n):
            part[j % 2, j // 2, :, cols] = value[j * r : (j + 1) * r]
        pair_copy(t).start()

    def q_tile(t, carry):
        qw_copy(t).wait()
        q_send(jnp.dot(hid_ref[...], qw_v[t], preferred_element_type=f32), t)
        return carry

    lax.fori_loop(0, tiles, q_tile, 0)
    kvw_copy.wait()
    q_send(jnp.dot(hid_ref[...], kvw_v[...], preferred_element_type=f32), tiles)

    def q_on(t, carry):
        cols = span_cols(t)
        pair_copy(t).wait_recv()
        part[parity, :, :, cols] = part[parity, :, :, cols] + qpair[:, :, cols]
        mates(
            lambda k, j: remote(
                part.at[parity, k, :, cols], qrecv.at[col, :, cols], q_s.at[k], q_r.at[col], {"seq": j}
            ).start()
        )
        return carry

    lax.fori_loop(0, tiles + 1, q_on, 0)

    holder = w == me // per_half

    def tok_recv(i, device):
        block = tokg.at[lax.rem(i, 2), i // 2]
        return remote(block, block, fwd_s.at[i], tok_r.at[i], device)

    @pl.when(holder)
    def _():
        pltpu.make_async_copy(tokg.at[parity, col], tokg.at[parity, col], own_sem).wait()

        def pass_on(d, carry):
            i = lax.rem(me + d, n)

            @pl.when(i != me)
            def _():
                tok_recv(i, {"seq": i}).wait_recv()

            tok_recv(i, {"width": other}).start()
            return carry

        lax.fori_loop(0, n, pass_on, 0)

    @pl.when(jnp.logical_not(holder))
    def _():
        def take(i, carry):
            tok_recv(i, {"width": other}).wait_recv()
            return carry

        lax.fori_loop(0, n, take, 0)

    group = min(half, 8)

    def span_part(side):
        def chunk(c, carry):
            rows = tokg[side, pl.ds(c * group, group)].reshape(group * toks, feats)
            value = jnp.dot(rows, kvw_v[...], preferred_element_type=f32)
            spart[side, pl.ds(c * group, group)] = value.reshape(group, toks, value.shape[1])
            return carry

        lax.fori_loop(0, half // group, chunk, 0)

    span_part(1 - parity)
    span_pair = remote(spart.at[1 - parity], spair, spp_s, spp_r, {"seq": pair})
    span_pair.start()
    span_part(parity)

    qrecv[col] = part[parity, col]
    mates(
        lambda k, j: remote(
            part.at[parity, k], qrecv.at[k], q_s.at[k], q_r.at[k], {"seq": j}
        ).wait_recv()
    )
    total = lax.fori_loop(1, half, lambda i, acc: acc + qrecv[i], qrecv[0])
    gath[me] = jnp.concatenate(
        [total[:, c * HD : (c + 1) * HD] for c in range(ccols // HD)], axis=0
    ).astype(bf16)
    spread(gath, g_s, gp_s, g_r)

    span_pair.wait_recv()
    spart[parity] = spart[parity] + spair[...]
    mates(
        lambda k, j: remote(
            spart.at[parity, k], srecv.at[col], sp_s.at[k], sp_r.at[col], {"seq": j}
        ).start()
    )
    relay(gath, g_s, gp_s, g_r)

    ck_copy.wait()
    cv_copy.wait()
    for h in range(heads):
        vt_v[h] = cv_v[:, h * HD : (h + 1) * HD].astype(f32).T.astype(bf16)

    srecv[col] = spart[parity, col]
    collect(gath, gp_s, g_r)

    slots = ck_v.shape[0]
    anchor = me * slots
    jc = max(1, min(n, 256 // lanes))
    width = jc * lanes

    def queries(c, h):
        return gath[pl.ds(c * jc, jc), h * lanes : (h + 1) * lanes, :].reshape(width, HD)

    def attend_cache(c, carry):
        visible = vis_ref[pl.ds(c, 1)] - anchor
        for h in range(heads):
            s = lax.dot_general(
                ck_v[:, h * HD : (h + 1) * HD], queries(c, h), NT, preferred_element_type=f32
            ) * factor
            place = lax.broadcasted_iota(jnp.int32, s.shape, 0)
            s = jnp.where(place < visible, s, MASKED)
            m = jnp.max(s, axis=0, keepdims=True)
            e = jnp.exp(s - m)
            mlacc[c, h : h + 1] = m
            mlacc[c, heads + h : heads + h + 1] = jnp.sum(e, axis=0, keepdims=True)
            oacc[c, h] = jnp.dot(vt_v[h], e.astype(bf16), preferred_element_type=f32)
        return carry

    lax.fori_loop(0, n // jc, attend_cache, 0)

    mates(
        lambda k, j: remote(
            spart.at[parity, k], srecv.at[k], sp_s.at[k], sp_r.at[k], {"seq": j}
        ).wait_recv()
    )
    span = lax.fori_loop(1, half, lambda i, acc: acc + srecv[i], srecv[0]).astype(bf16)
    span_ref[...] = span
    for h in range(heads):
        vts_v[h] = span[:, (2 * h + 1) * HD : (2 * h + 2) * HD].astype(f32).T.astype(bf16)

    def attend_span(c, carry):
        for h in range(heads):
            s = lax.dot_general(
                span_ref[:, 2 * h * HD : (2 * h + 1) * HD], queries(c, h), NT, preferred_element_type=f32
            ) * factor
            m0 = mlacc[c, h : h + 1]
            m = jnp.maximum(m0, jnp.max(s, axis=0, keepdims=True))
            keep = jnp.exp(m0 - m)
            e = jnp.exp(s - m)
            l = mlacc[c, heads + h : heads + h + 1] * keep + jnp.sum(e, axis=0, keepdims=True)
            o = jnp.dot(vts_v[h], e.astype(bf16), preferred_element_type=f32)
            o = (oacc[c, h] * keep + o).astype(bf16)
            for k in range(jc):
                cut = slice(k * lanes, (k + 1) * lanes)
                obuf[c * jc + k, h] = o[:, cut]
                mlbuf[c * jc + k, h : h + 1] = m[:, cut]
                mlbuf[c * jc + k, heads + h : heads + h + 1] = l[:, cut]
        for k in range(jc):
            j = c * jc + k

            @pl.when(j != me)
            def _():
                remote(mlbuf.at[j], mlrecv.at[me], ml_s.at[j], ml_r.at[me], {"seq": j}).start()
                remote(obuf.at[j], orecv.at[me], o_s.at[j], o_r.at[me], {"seq": j}).start()

        return carry

    lax.fori_loop(0, n // jc, attend_span, 0)

    per_step = n // steps
    step = me // per_step
    fresh = []
    for h in range(heads):
        q = gath[me, h * lanes : (h + 1) * lanes, :]
        base = (heads * grouped + 2 * h) * r
        pairs = [
            gath[u * per_step + lax.rem(me, per_step)].astype(f32) for u in range(steps)
        ]
        keys = jnp.concatenate([p[base : base + r] for p in pairs], axis=0)
        values = jnp.concatenate([p[base + r : base + 2 * r] for p in pairs], axis=0)
        s = lax.dot_general(keys.astype(bf16), q, NT, preferred_element_type=f32) * factor
        row = lax.broadcasted_iota(jnp.int32, s.shape, 0)
        lane = lax.broadcasted_iota(jnp.int32, s.shape, 1)
        allowed = jnp.logical_and(lax.rem(row, r) == lax.rem(lane, r), row // r <= step)
        s = jnp.where(allowed, s, MASKED)
        m = jnp.max(s, axis=0, keepdims=True)
        e = jnp.where(allowed, jnp.exp(s - m), 0.0)
        l = jnp.sum(e, axis=0, keepdims=True)
        o = jnp.dot(values.T.astype(bf16), e.astype(bf16), preferred_element_type=f32)
        fresh.append((m, l, o))

    orecv[me] = obuf[me]
    mlrecv[me] = mlbuf[me]

    def o_wait(j):
        remote(mlbuf.at[j], mlrecv.at[j], ml_s.at[j], ml_r.at[j], {"seq": j}).wait_recv()
        remote(obuf.at[j], orecv.at[j], o_s.at[j], o_r.at[j], {"seq": j}).wait_recv()

    peers(o_wait)
    pieces = []
    for h in range(heads):
        m0, l0, o0 = fresh[h]
        top = lax.fori_loop(0, n, lambda i, a: jnp.maximum(a, mlrecv[i, h : h + 1]), m0)
        keep = jnp.exp(m0 - top)

        def fold(i, acc):
            k = jnp.exp(mlrecv[i, h : h + 1] - top)
            return acc[0] + mlrecv[i, heads + h : heads + h + 1] * k, acc[1] + orecv[i, h].astype(f32) * k

        l, o = lax.fori_loop(0, n, fold, (l0 * keep, o0 * keep))
        ready = (o / l).T
        pieces += [ready[g * r : (g + 1) * r] for g in range(grouped)]
    att[me] = jnp.concatenate(pieces, axis=1).astype(bf16)
    spread(att, a_s, ap_s, a_r)
    for copy in ow_copies:
        copy.wait()
    relay(att, a_s, ap_s, a_r)
    collect(att, ap_s, a_r)
    rows = jnp.concatenate([att[j].astype(f32) for j in range(n)], axis=0).astype(bf16)
    own = out_ref.shape[1]
    cut = min(own, 256)

    def out_tile(side, c):
        cols = pl.ds(pl.multiple_of(side * own + c * cut, 128), cut)
        return jnp.dot(rows, ow_v[:, cols], preferred_element_type=f32)

    for c in range(own // cut):
        xbuf[:, c * cut : (c + 1) * cut] = out_tile(other, c).astype(bf16)
    swap = remote(xbuf, xrecv, x_s, x_r, {"width": other})
    swap.start()
    kept = [out_tile(w, c) for c in range(own // cut)]
    swap.wait_recv()
    for c in range(own // cut):
        there = slice(c * cut, (c + 1) * cut)
        out_ref[:, there] = (kept[c] + xrecv[:, there].astype(f32)).astype(bf16)

    def tok_sent(k, carry):
        dest, cols = tok_copy(k)

        @pl.when(dest != me)
        def _():
            remote(
                tok_ref.at[:, cols], tokg.at[parity, col], tok_s.at[k], tok_r.at[me], {"seq": dest}
            ).wait_send()

        return carry

    lax.fori_loop(0, per_half, tok_sent, 0)

    @pl.when(holder)
    def _():
        def passed(i, carry):
            tok_recv(i, {"width": other}).wait_send()
            return carry

        lax.fori_loop(0, n, passed, 0)

    def pair_sent(t, carry):
        pair_copy(t).wait_send()
        return carry

    lax.fori_loop(0, tiles + 1, pair_sent, 0)
    span_pair.wait_send()

    def sums_sent(k, j):
        at = {"seq": j}
        remote(part.at[parity, k], qrecv.at[col], q_s.at[k], q_r.at[col], at).wait_send()
        remote(spart.at[parity, k], srecv.at[col], sp_s.at[k], sp_r.at[col], at).wait_send()

    mates(sums_sent)
    spread_sent(gath, g_s, gp_s, g_r)
    spread_sent(att, a_s, ap_s, a_r)

    def sent(j):
        at = {"seq": j}
        remote(mlbuf.at[j], mlrecv.at[me], ml_s.at[j], ml_r.at[me], at).wait_send()
        remote(obuf.at[j], orecv.at[me], o_s.at[j], o_r.at[me], at).wait_send()

    peers(sent)
    swap.wait_send()


def local(
    mesh,
    span_tokens, kv_weight, query_weight, out_weight, cache_keys, cache_values, hidden, lengths, offset,
):
    n = mesh.shape["seq"]
    steps, branches, feats = hidden.shape
    rows = steps * branches
    r = rows // n
    grouped = QH // KVH
    lanes = grouped * r
    toks = span_tokens.shape[0]
    kvc = kv_weight.shape[1]
    heads = kvc // (2 * HD)
    qcols = query_weight.shape[1]
    ccols = qcols + kvc
    tile = kvc
    half = n // 2
    slots = cache_keys.shape[0]
    own = out_weight.shape[1] // mesh.shape["width"]
    f32, bf16 = jnp.float32, jnp.bfloat16

    jc = max(1, min(n, 256 // lanes))
    visible = jnp.tile(jnp.minimum(lengths, offset[0]), steps).reshape(n, 1, r)
    visible = jnp.broadcast_to(visible, (n, grouped, r)).reshape(n // jc, jc * lanes)

    vm = pl.BlockSpec(memory_space=pltpu.VMEM)
    hbm = pl.BlockSpec(memory_space=pl.ANY)
    dma = pltpu.SemaphoreType.DMA
    ow_parts = 8
    span_kv, out = pl.pallas_call(
        functools.partial(layer, n, steps, tile),
        out_shape=(
            jax.ShapeDtypeStruct((toks, kvc), bf16),
            jax.ShapeDtypeStruct((rows, own), bf16),
        ),
        in_specs=[vm, vm, vm, hbm, hbm, hbm, hbm, hbm],
        out_specs=(vm, vm),
        scratch_shapes=[
            pltpu.VMEM((qcols // tile, feats, tile), bf16),
            pltpu.VMEM((feats, kvc), bf16),
            pltpu.VMEM(out_weight.shape, bf16),
            pltpu.VMEM((slots, heads * HD), bf16),
            pltpu.VMEM((slots, heads * HD), bf16),
            pltpu.VMEM((heads, HD, slots), bf16),
            pltpu.VMEM((heads, HD, toks), bf16),
            pltpu.VMEM((2, half, r, ccols), f32),
            pltpu.VMEM((half, r, ccols), f32),
            pltpu.VMEM((half, r, ccols), f32),
            pltpu.VMEM((2, half, toks, feats), bf16),
            pltpu.VMEM((2, half, toks, kvc), f32),
            pltpu.VMEM((half, toks, kvc), f32),
            pltpu.VMEM((half, toks, kvc), f32),
            pltpu.VMEM((n, ccols // HD * r, HD), bf16),
            pltpu.VMEM((n // jc, heads, HD, jc * lanes), f32),
            pltpu.VMEM((n // jc, 2 * heads, jc * lanes), f32),
            pltpu.VMEM((n, heads, HD, lanes), bf16),
            pltpu.VMEM((n, heads, HD, lanes), bf16),
            pltpu.VMEM((n, 2 * heads, lanes), f32),
            pltpu.VMEM((n, 2 * heads, lanes), f32),
            pltpu.VMEM((n, r, qcols), bf16),
            pltpu.VMEM((rows, own), bf16),
            pltpu.VMEM((rows, own), bf16),
            dma((qcols // tile,)), dma, dma((ow_parts,)), dma((2,)), dma,
            dma((n,)), dma((n,)), dma((n,)),
            dma((qcols // tile + 1,)), dma((qcols // tile + 1,)), dma((half,)), dma((half,)),
            dma, dma, dma((half,)), dma((half,)),
            dma((half,)), dma((n,)), dma((half,)),
            dma((n,)), dma((n,)), dma((n,)), dma((n,)),
            dma((half,)), dma((n,)), dma((half,)),
            dma, dma,
        ],
        compiler_params=pltpu.CompilerParams(
            collective_id=0, has_side_effects=True, vmem_limit_bytes=62 * 1024 * 1024
        ),
    )(
        span_tokens,
        hidden.reshape(rows, feats),
        visible,
        kv_weight,
        query_weight,
        out_weight,
        cache_keys.reshape(slots, heads * HD),
        cache_values.reshape(slots, heads * HD),
    )
    return span_kv, out.reshape(steps, branches, own)


def solution(mesh):
    return jax.shard_map(
        functools.partial(local, mesh),
        mesh=mesh,
        in_specs=(
            P(("groups", "seq"), "width"),
            P("seq", "width"),
            P("seq", "width"),
            P("width", "seq"),
            P(("groups", "seq"), "width", None),
            P(("groups", "seq"), "width", None),
            P(None, "groups", "seq"),
            P("groups"),
            P("groups"),
        ),
        out_specs=(P(("groups", "seq"), "width"), P(None, "groups", ("seq", "width"))),
        check_vma=False,
    )
```

```python
import functools
import math

import jax
import jax.numpy as jnp
from jax import lax
from jax.experimental import pallas as pl
from jax.experimental.pallas import tpu as pltpu
from jax.sharding import PartitionSpec as P

HD = 128
QH = 64
KVH = 4
MASKED = -1e30
MESH = pl.DeviceIdType.MESH
NT = (((1,), (1,)), ((), ()))


def remote(src, dst, send, recv, device):
    return pltpu.make_async_remote_copy(
        src_ref=src, dst_ref=dst, send_sem=send, recv_sem=recv, device_id=device, device_id_type=MESH
    )


def layer(
    n, steps, tile,
    tok_ref, hid_ref, vis_ref, kvw_ref, qw_ref, ow_ref, ck_ref, cv_ref,
    span_ref, out_ref,
    qw_v, kvw_v, ow_v, ck_v, cv_v, kh_v, vt_v, vts_v,
    part, qpair, qrecv, tokg, spart, spair, srecv, gath,
    obuf, orecv, mlbuf, mlrecv, att, xbuf, xrecv,
    qw_sem, kvw_sem, ow_sem, c_sem, own_sem,
    tok_s, tok_r, fwd_s, qp_s, qp_r, q_s, q_r, spp_s, spp_r, sp_s, sp_r,
    g_s, g_r, gp_s, o_s, o_r, ml_s, ml_r, a_s, a_r, ap_s, x_s, x_r,
):
    f32, bf16 = jnp.float32, jnp.bfloat16
    me = lax.axis_index("seq")
    w = lax.axis_index("width")
    other = 1 - w
    parity, col, half = lax.rem(me, 2), me // 2, n // 2
    pair = me + 1 - 2 * parity
    r = part.shape[2]
    heads = kvw_v.shape[1] // (2 * HD)
    grouped = QH // KVH
    qcols = qw_ref.shape[1]
    ccols = part.shape[3]
    tiles = qcols // tile
    feats = hid_ref.shape[1]
    lanes = grouped * r
    factor = 1.0 / math.sqrt(HD)
    per_half = tok_ref.shape[1] // feats
    toks = tok_ref.shape[0]

    def peers(body):
        def step(d, carry):
            body(lax.rem(me + d, n))
            return carry

        lax.fori_loop(1, n, step, 0)

    def mates(body):
        def step(d, carry):
            k = lax.rem(col + d, half)
            body(k, 2 * k + parity)
            return carry

        lax.fori_loop(1, half, step, 0)

    def spread(buf, send, pass_on, recv):
        at_pair = {"seq": pair}
        mates(lambda k, j: remote(buf.at[me], buf.at[me], send.at[k], recv.at[me], {"seq": j}).start())
        remote(buf.at[me], buf.at[me], pass_on.at[col], recv.at[me], at_pair).start()

    def relay(buf, send, pass_on, recv):
        def one(k, j):
            remote(buf.at[j], buf.at[j], send.at[k], recv.at[j], {"seq": j}).wait_recv()
            remote(buf.at[j], buf.at[j], pass_on.at[k], recv.at[j], {"seq": pair}).start()

        mates(one)

    def collect(buf, pass_on, recv):
        def one(k, carry):
            j = 2 * k + 1 - parity
            remote(buf.at[j], buf.at[j], pass_on.at[k], recv.at[j], {"seq": pair}).wait_recv()
            return carry

        lax.fori_loop(0, half, one, 0)

    def spread_sent(buf, send, pass_on, recv):
        mates(
            lambda k, j: remote(buf.at[me], buf.at[me], send.at[k], recv.at[me], {"seq": j}).wait_send()
        )

        def one(k, carry):
            j = 2 * k + parity
            remote(buf.at[j], buf.at[j], pass_on.at[k], recv.at[j], {"seq": pair}).wait_send()
            return carry

        lax.fori_loop(0, half, one, 0)

    def qw_copy(t):
        cols = pl.ds(pl.multiple_of(t * tile, tile), tile)
        return pltpu.make_async_copy(qw_ref.at[:, cols], qw_v.at[t], qw_sem.at[t])

    for t in range(tiles):
        qw_copy(t).start()
    kvw_copy = pltpu.make_async_copy(kvw_ref, kvw_v, kvw_sem)
    kvw_copy.start()
    ck_copy = pltpu.make_async_copy(ck_ref, ck_v, c_sem.at[0])
    cv_copy = pltpu.make_async_copy(cv_ref, cv_v, c_sem.at[1])
    ck_copy.start()
    cv_copy.start()
    ow_parts = ow_sem.shape[0]
    ow_rows = ow_ref.shape[0] // ow_parts
    ow_copies = [
        pltpu.make_async_copy(
            ow_ref.at[pl.ds(k * ow_rows, ow_rows)], ow_v.at[pl.ds(k * ow_rows, ow_rows)], ow_sem.at[k]
        )
        for k in range(ow_parts)
    ]
    for copy in ow_copies:
        copy.start()

    barrier = pltpu.get_barrier_semaphore()
    peers(
        lambda j: pl.semaphore_signal(barrier, inc=1, device_id={"seq": j}, device_id_type=MESH)
    )
    pl.semaphore_signal(barrier, inc=1, device_id={"width": other}, device_id_type=MESH)
    pl.semaphore_wait(barrier, n)

    def tok_copy(k):
        dest = w * per_half + k
        cols = pl.ds(pl.multiple_of(k * feats, 128), feats)
        return dest, cols

    def tok_send(k, carry):
        dest, cols = tok_copy(k)

        @pl.when(dest != me)
        def _():
            remote(
                tok_ref.at[:, cols], tokg.at[parity, col], tok_s.at[k], tok_r.at[me], {"seq": dest}
            ).start()

        @pl.when(dest == me)
        def _():
            pltpu.make_async_copy(tok_ref.at[:, cols], tokg.at[parity, col], own_sem).start()

        return carry

    lax.fori_loop(0, per_half, tok_send, 0)

    def span_cols(t):
        return pl.ds(pl.multiple_of(t * tile, tile), tile)

    def pair_copy(t):
        cols = span_cols(t)
        return remote(
            part.at[1 - parity, :, :, cols], qpair.at[:, :, cols], qp_s.at[t], qp_r.at[t], {"seq": pair}
        )

    def q_send(value, t):
        cols = span_cols(t)
        for j in range(n):
            part[j % 2, j // 2, :, cols] = value[j * r : (j + 1) * r]
        pair_copy(t).start()

    def q_on(t, carry):
        cols = span_cols(t)
        pair_copy(t).wait_recv()
        part[parity, :, :, cols] = part[parity, :, :, cols] + qpair[:, :, cols]
        mates(
            lambda k, j: remote(
                part.at[parity, k, :, cols], qrecv.at[col, :, cols], q_s.at[k], q_r.at[col], {"seq": j}
            ).start()
        )
        return carry

    lag = 3

    def q_tile(t, carry):
        qw_copy(t).wait()
        q_send(jnp.dot(hid_ref[...], qw_v[t], preferred_element_type=f32), t)

        @pl.when(t >= lag)
        def _():
            q_on(t - lag, 0)

        return carry

    lax.fori_loop(0, tiles, q_tile, 0)
    kvw_copy.wait()
    q_send(jnp.dot(hid_ref[...], kvw_v[...], preferred_element_type=f32), tiles)

    lax.fori_loop(max(tiles - lag, 0), tiles + 1, q_on, 0)

    holder = w == me // per_half

    def tok_recv(i, device):
        block = tokg.at[lax.rem(i, 2), i // 2]
        return remote(block, block, fwd_s.at[i], tok_r.at[i], device)

    @pl.when(holder)
    def _():
        pltpu.make_async_copy(tokg.at[parity, col], tokg.at[parity, col], own_sem).wait()

        def pass_on(d, carry):
            i = lax.rem(me + d, n)

            @pl.when(i != me)
            def _():
                tok_recv(i, {"seq": i}).wait_recv()

            tok_recv(i, {"width": other}).start()
            return carry

        lax.fori_loop(0, n, pass_on, 0)

    @pl.when(jnp.logical_not(holder))
    def _():
        def take(i, carry):
            tok_recv(i, {"width": other}).wait_recv()
            return carry

        lax.fori_loop(0, n, take, 0)

    group = min(half, 8)

    def span_part(side):
        def chunk(c, carry):
            rows = tokg[side, pl.ds(c * group, group)].reshape(group * toks, feats)
            value = jnp.dot(rows, kvw_v[...], preferred_element_type=f32)
            spart[side, pl.ds(c * group, group)] = value.reshape(group, toks, value.shape[1])
            return carry

        lax.fori_loop(0, half // group, chunk, 0)

    span_part(1 - parity)
    span_pair = remote(spart.at[1 - parity], spair, spp_s, spp_r, {"seq": pair})
    span_pair.start()
    span_part(parity)

    ck_copy.wait()
    cv_copy.wait()
    for h in range(heads):
        vt_v[h] = cv_v[...].astype(f32)[:, h, :].T.astype(bf16)
        kh_v[h] = ck_v[...].astype(f32)[:, h, :].astype(bf16)

    qrecv[col] = part[parity, col]
    mates(
        lambda k, j: remote(
            part.at[parity, k], qrecv.at[k], q_s.at[k], q_r.at[k], {"seq": j}
        ).wait_recv()
    )
    total = lax.fori_loop(1, half, lambda i, acc: acc + qrecv[i], qrecv[0])
    gath[me] = jnp.concatenate(
        [total[:, c * HD : (c + 1) * HD] for c in range(ccols // HD)], axis=0
    ).astype(bf16)
    spread(gath, g_s, gp_s, g_r)

    span_pair.wait_recv()
    spart[parity] = spart[parity] + spair[...]
    mates(
        lambda k, j: remote(
            spart.at[parity, k], srecv.at[col], sp_s.at[k], sp_r.at[col], {"seq": j}
        ).start()
    )
    relay(gath, g_s, gp_s, g_r)

    srecv[col] = spart[parity, col]
    collect(gath, gp_s, g_r)

    slots = ck_v.shape[0]
    anchor = me * slots
    jc = max(1, min(n, 256 // lanes))
    width = jc * lanes

    def queries(c, h):
        return gath[pl.ds(c * jc, jc), h * lanes : (h + 1) * lanes, :].reshape(width, HD)

    mates(
        lambda k, j: remote(
            spart.at[parity, k], srecv.at[k], sp_s.at[k], sp_r.at[k], {"seq": j}
        ).wait_recv()
    )
    span = lax.fori_loop(1, half, lambda i, acc: acc + srecv[i], srecv[0]).astype(bf16)
    span_ref[...] = span
    for h in range(heads):
        vts_v[h] = span[:, (2 * h + 1) * HD : (2 * h + 2) * HD].astype(f32).T.astype(bf16)

    def attend(i, carry):
        c = lax.rem(me // jc + 1 + i, n // jc)
        visible = vis_ref[pl.ds(c, 1)] - anchor
        for h in range(heads):
            q = queries(c, h)
            s1 = lax.dot_general(kh_v[h], q, NT, preferred_element_type=f32) * factor
            s2 = lax.dot_general(
                span_ref[:, 2 * h * HD : (2 * h + 1) * HD], q, NT, preferred_element_type=f32
            ) * factor
            place = lax.broadcasted_iota(jnp.int32, s1.shape, 0)
            s1 = jnp.where(place < visible, s1, MASKED)
            m = jnp.maximum(
                jnp.max(s1, axis=0, keepdims=True), jnp.max(s2, axis=0, keepdims=True)
            )
            w1 = jnp.exp(s1 - m)
            w2 = jnp.exp(s2 - m)
            l = jnp.sum(w1, axis=0, keepdims=True) + jnp.sum(w2, axis=0, keepdims=True)
            o = jnp.dot(vt_v[h], w1.astype(bf16), preferred_element_type=f32)
            o = (o + jnp.dot(vts_v[h], w2.astype(bf16), preferred_element_type=f32)).astype(bf16)
            for k in range(jc):
                cut = slice(k * lanes, (k + 1) * lanes)
                obuf[c * jc + k, h] = o[:, cut]
                mlbuf[c * jc + k, h : h + 1] = m[:, cut]
                mlbuf[c * jc + k, heads + h : heads + h + 1] = l[:, cut]
        for k in range(jc):
            j = c * jc + k

            @pl.when(j != me)
            def _():
                remote(mlbuf.at[j], mlrecv.at[me], ml_s.at[j], ml_r.at[me], {"seq": j}).start()
                remote(obuf.at[j], orecv.at[me], o_s.at[j], o_r.at[me], {"seq": j}).start()

        return carry

    lax.fori_loop(0, n // jc, attend, 0)

    per_step = n // steps
    step = me // per_step
    fresh = []
    for h in range(heads):
        q = gath[me, h * lanes : (h + 1) * lanes, :]
        base = (heads * grouped + 2 * h) * r
        pairs = [
            gath[u * per_step + lax.rem(me, per_step)].astype(f32) for u in range(steps)
        ]
        keys = jnp.concatenate([p[base : base + r] for p in pairs], axis=0)
        values = jnp.concatenate([p[base + r : base + 2 * r] for p in pairs], axis=0)
        s = lax.dot_general(keys.astype(bf16), q, NT, preferred_element_type=f32) * factor
        row = lax.broadcasted_iota(jnp.int32, s.shape, 0)
        lane = lax.broadcasted_iota(jnp.int32, s.shape, 1)
        allowed = jnp.logical_and(lax.rem(row, r) == lax.rem(lane, r), row // r <= step)
        s = jnp.where(allowed, s, MASKED)
        m = jnp.max(s, axis=0, keepdims=True)
        e = jnp.where(allowed, jnp.exp(s - m), 0.0)
        l = jnp.sum(e, axis=0, keepdims=True)
        o = jnp.dot(values.T.astype(bf16), e.astype(bf16), preferred_element_type=f32)
        fresh.append((m, l, o))

    orecv[me] = obuf[me]
    mlrecv[me] = mlbuf[me]

    def o_wait(j):
        remote(mlbuf.at[j], mlrecv.at[j], ml_s.at[j], ml_r.at[j], {"seq": j}).wait_recv()
        remote(obuf.at[j], orecv.at[j], o_s.at[j], o_r.at[j], {"seq": j}).wait_recv()

    peers(o_wait)
    pieces = []
    for h in range(heads):
        m0, l0, o0 = fresh[h]
        tops, sums = mlrecv[:, h, :], mlrecv[:, heads + h, :]
        top = jnp.maximum(m0, jnp.max(tops, axis=0, keepdims=True))
        keep = jnp.exp(m0 - top)
        weight = jnp.exp(tops - top)
        l = l0 * keep + jnp.sum(sums * weight, axis=0, keepdims=True)
        o = o0 * keep
        for i in range(n):
            o = o + orecv[i, h].astype(f32) * weight[i : i + 1]
        ready = (o / l).T
        pieces += [ready[g * r : (g + 1) * r] for g in range(grouped)]
    att[me] = jnp.concatenate(pieces, axis=1).astype(bf16)
    spread(att, a_s, ap_s, a_r)
    for copy in ow_copies:
        copy.wait()
    relay(att, a_s, ap_s, a_r)
    collect(att, ap_s, a_r)
    rows = jnp.concatenate([att[j].astype(f32) for j in range(n)], axis=0).astype(bf16)
    own = out_ref.shape[1]
    cut = min(own, 256)

    def out_tile(side, c):
        cols = pl.ds(pl.multiple_of(side * own + c * cut, 128), cut)
        return jnp.dot(rows, ow_v[:, cols], preferred_element_type=f32)

    for c in range(own // cut):
        xbuf[:, c * cut : (c + 1) * cut] = out_tile(other, c).astype(bf16)
    swap = remote(xbuf, xrecv, x_s, x_r, {"width": other})
    swap.start()
    kept = [out_tile(w, c) for c in range(own // cut)]
    swap.wait_recv()
    for c in range(own // cut):
        there = slice(c * cut, (c + 1) * cut)
        out_ref[:, there] = (kept[c] + xrecv[:, there].astype(f32)).astype(bf16)

    def tok_sent(k, carry):
        dest, cols = tok_copy(k)

        @pl.when(dest != me)
        def _():
            remote(
                tok_ref.at[:, cols], tokg.at[parity, col], tok_s.at[k], tok_r.at[me], {"seq": dest}
            ).wait_send()

        return carry

    lax.fori_loop(0, per_half, tok_sent, 0)

    @pl.when(holder)
    def _():
        def passed(i, carry):
            tok_recv(i, {"width": other}).wait_send()
            return carry

        lax.fori_loop(0, n, passed, 0)

    def pair_sent(t, carry):
        pair_copy(t).wait_send()
        return carry

    lax.fori_loop(0, tiles + 1, pair_sent, 0)
    span_pair.wait_send()

    def sums_sent(k, j):
        at = {"seq": j}
        remote(part.at[parity, k], qrecv.at[col], q_s.at[k], q_r.at[col], at).wait_send()
        remote(spart.at[parity, k], srecv.at[col], sp_s.at[k], sp_r.at[col], at).wait_send()

    mates(sums_sent)
    spread_sent(gath, g_s, gp_s, g_r)
    spread_sent(att, a_s, ap_s, a_r)

    def sent(j):
        at = {"seq": j}
        remote(mlbuf.at[j], mlrecv.at[me], ml_s.at[j], ml_r.at[me], at).wait_send()
        remote(obuf.at[j], orecv.at[me], o_s.at[j], o_r.at[me], at).wait_send()

    peers(sent)
    swap.wait_send()


def local(
    mesh,
    span_tokens, kv_weight, query_weight, out_weight, cache_keys, cache_values, hidden, lengths, offset,
):
    n = mesh.shape["seq"]
    steps, branches, feats = hidden.shape
    rows = steps * branches
    r = rows // n
    grouped = QH // KVH
    lanes = grouped * r
    toks = span_tokens.shape[0]
    kvc = kv_weight.shape[1]
    heads = kvc // (2 * HD)
    qcols = query_weight.shape[1]
    ccols = qcols + kvc
    tile = kvc
    half = n // 2
    slots = cache_keys.shape[0]
    own = out_weight.shape[1] // mesh.shape["width"]
    f32, bf16 = jnp.float32, jnp.bfloat16

    jc = max(1, min(n, 256 // lanes))
    visible = jnp.tile(jnp.minimum(lengths, offset[0]), steps).reshape(n, 1, r)
    visible = jnp.broadcast_to(visible, (n, grouped, r)).reshape(n // jc, jc * lanes)

    vm = pl.BlockSpec(memory_space=pltpu.VMEM)
    hbm = pl.BlockSpec(memory_space=pl.ANY)
    dma = pltpu.SemaphoreType.DMA
    ow_parts = 8
    span_kv, out = pl.pallas_call(
        functools.partial(layer, n, steps, tile),
        out_shape=(
            jax.ShapeDtypeStruct((toks, kvc), bf16),
            jax.ShapeDtypeStruct((rows, own), bf16),
        ),
        in_specs=[vm, vm, vm, hbm, hbm, hbm, hbm, hbm],
        out_specs=(vm, vm),
        scratch_shapes=[
            pltpu.VMEM((qcols // tile, feats, tile), bf16),
            pltpu.VMEM((feats, kvc), bf16),
            pltpu.VMEM(out_weight.shape, bf16),
            pltpu.VMEM((slots, heads, HD), bf16),
            pltpu.VMEM((slots, heads, HD), bf16),
            pltpu.VMEM((heads, slots, HD), bf16),
            pltpu.VMEM((heads, HD, slots), bf16),
            pltpu.VMEM((heads, HD, toks), bf16),
            pltpu.VMEM((2, half, r, ccols), f32),
            pltpu.VMEM((half, r, ccols), f32),
            pltpu.VMEM((half, r, ccols), f32),
            pltpu.VMEM((2, half, toks, feats), bf16),
            pltpu.VMEM((2, half, toks, kvc), f32),
            pltpu.VMEM((half, toks, kvc), f32),
            pltpu.VMEM((half, toks, kvc), f32),
            pltpu.VMEM((n, ccols // HD * r, HD), bf16),
            pltpu.VMEM((n, heads, HD, lanes), bf16),
            pltpu.VMEM((n, heads, HD, lanes), bf16),
            pltpu.VMEM((n, 2 * heads, lanes), f32),
            pltpu.VMEM((n, 2 * heads, lanes), f32),
            pltpu.VMEM((n, r, qcols), bf16),
            pltpu.VMEM((rows, own), bf16),
            pltpu.VMEM((rows, own), bf16),
            dma((qcols // tile,)), dma, dma((ow_parts,)), dma((2,)), dma,
            dma((n,)), dma((n,)), dma((n,)),
            dma((qcols // tile + 1,)), dma((qcols // tile + 1,)), dma((half,)), dma((half,)),
            dma, dma, dma((half,)), dma((half,)),
            dma((half,)), dma((n,)), dma((half,)),
            dma((n,)), dma((n,)), dma((n,)), dma((n,)),
            dma((half,)), dma((n,)), dma((half,)),
            dma, dma,
        ],
        compiler_params=pltpu.CompilerParams(
            collective_id=0, has_side_effects=True, vmem_limit_bytes=62 * 1024 * 1024
        ),
    )(
        span_tokens,
        hidden.reshape(rows, feats),
        visible,
        kv_weight,
        query_weight,
        out_weight,
        cache_keys,
        cache_values,
    )
    return span_kv, out.reshape(steps, branches, own)


def solution(mesh):
    return jax.shard_map(
        functools.partial(local, mesh),
        mesh=mesh,
        in_specs=(
            P(("groups", "seq"), "width"),
            P("seq", "width"),
            P("seq", "width"),
            P("width", "seq"),
            P(("groups", "seq"), "width", None),
            P(("groups", "seq"), "width", None),
            P(None, "groups", "seq"),
            P("groups"),
            P("groups"),
        ),
        out_specs=(P(("groups", "seq"), "width"), P(None, "groups", ("seq", "width"))),
        check_vma=False,
    )
```
